32 devices in a mesh: dp: 4 (over z), ctx: 2 (over x), hidden: 4 (over y, core).
Axes of the slice: x: 2, y: 2, z: 4, core: 2. Of those that a mesh axis runs over, the one named last changes fastest.
Arguments:
- activations: bfloat16 [4, 1024, 53248], P('dp', 'ctx', 'hidden'), may hold values from -6 to 6
- out_grads: bfloat16 [4, 1024, 16384], P('dp', 'ctx', 'hidden'), may hold values from -0.1875 to 0.1875
- input_basis: bfloat16 [53248, 512], P('hidden', ('dp', 'ctx')), may hold values from -0.02734375 to 0.02734375
- output_basis: bfloat16 [16384, 512], P('hidden', ('dp', 'ctx')), may hold values from -0.046875 to 0.046875
- rotation: bfloat16 [512, 512], P('ctx'), may hold values from -0.25 to 0.25
Outputs:
- logged: float32 [4, 512, 512], P('dp', 'ctx', 'hidden')
The draws below stay inside these ranges and needn't reach their ends.
All inputs are finite; a program needn't handle non-finite values.
Results may differ from the reference program's by a relative error of at most 0.0049.
Values may be sent and summed in bfloat16 or wider, within the bound.
A program may use at most 64 MiB of HBM per device.

```python
import jax
import jax.numpy as jnp
from jax import lax

DIN = 53248
DOUT = 16384
RANK = 512
SEQLEN = 1024
SEQS = 4


def steps_of(own_key, extent, pieces, low, top_value):
    def one(position, blocks):
        draws = jax.random.uniform(jax.random.fold_in(jax.random.fold_in(own_key, 6), position), (blocks,), jnp.float32, low / len(pieces), top_value / len(pieces))
        return jnp.repeat(jnp.exp(draws), extent[position] // blocks).reshape((-1,) + (1,) * (len(extent) - position - 1))

    loudness = one(*pieces[0])
    for cut in pieces[1:]:
        loudness = loudness * one(*cut)
    return loudness


def bell_draw(key, extent, width, reach, pieces=(), kind=jnp.bfloat16):
    gain = steps_of(key, extent, pieces, -0.22, 0.18) if pieces else 1.0
    result = jax.random.normal(key, extent, jnp.float32) * width * gain
    return jnp.minimum(jnp.maximum(result, -reach), reach).astype(kind)


def setup_inputs(seed: int = 0) -> dict:
    seeds = jax.random.split(jax.random.key(seed), 6)
    return {
        "activations": bell_draw(seeds[0], (SEQS, SEQLEN, DIN), 1.0, 6.0, ((0, 4), (1, 2), (2, 4))),
        "out_grads": bell_draw(seeds[1], (SEQS, SEQLEN, DOUT), SEQLEN ** -0.5, 0.1875, ((0, 4), (1, 2), (2, 4))),
        "input_basis": bell_draw(seeds[2], (DIN, RANK), DIN ** -0.5, 0.02734375, ((0, 4), (1, 8))),
        "output_basis": bell_draw(seeds[3], (DOUT, RANK), DOUT ** -0.5, 0.046875, ((0, 4), (1, 8))),
        "rotation": bell_draw(seeds[4], (RANK, RANK), RANK ** -0.5, 0.25, ((0, 2),)),
    }


def reference(activations, out_grads, input_basis, output_basis, rotation):
    def one_sequence(pair):
        tokens, grad_rows = pair
        in_side = jnp.dot(tokens, input_basis, preferred_element_type=jnp.float32).astype(jnp.bfloat16)
        out_side = jnp.dot(grad_rows, output_basis, preferred_element_type=jnp.float32).astype(jnp.bfloat16)
        total = jnp.dot(out_side.T, in_side, preferred_element_type=jnp.float32)
        lowrank = total.astype(jnp.bfloat16)
        return jnp.dot(rotation, lowrank, preferred_element_type=jnp.float32)

    return lax.map(one_sequence, (activations, out_grads))
```

```python
import functools

import jax
import jax.numpy as jnp
from jax import lax
from jax.experimental import pallas as pl
from jax.experimental.pallas import tpu as pltpu
from jax.sharding import PartitionSpec as P

MESH = pl.DeviceIdType.MESH
NT = (((1,), (1,)), ((), ()))
CHUNK = 1024
NZ = 4
LAG = 1


def outer_sum(left, right):
    return lax.dot_general(
        left, right, (((0,), (0,)), ((), ())), preferred_element_type=jnp.float32
    )


def local(activations, out_grads, input_basis, output_basis, rotation):
    tokens = activations.reshape(-1, activations.shape[-1])
    grad_rows = out_grads.reshape(-1, out_grads.shape[-1])
    in_part = jnp.dot(
        tokens,
        lax.all_gather(input_basis, ("dp", "ctx"), axis=1, tiled=True),
        preferred_element_type=jnp.float32,
    )
    out_part = jnp.dot(
        grad_rows,
        lax.all_gather(output_basis, ("dp", "ctx"), axis=1, tiled=True),
        preferred_element_type=jnp.float32,
    )
    in_cols = lax.psum_scatter(in_part, "hidden", scatter_dimension=1, tiled=True).astype(
        jnp.bfloat16
    )
    out_side = lax.psum(out_part, "hidden")
    out_side = out_side.astype(jnp.bfloat16)
    total = lax.psum(outer_sum(out_side, in_cols), "ctx")
    lowrank = total.astype(jnp.bfloat16)
    logged = jnp.dot(rotation, lowrank, preferred_element_type=jnp.float32)
    return logged.reshape(1, logged.shape[0], logged.shape[1])


def kernel(
    n_out, n_in, n_a,
    act_hbm, grad_hbm, bi_hbm, bo_hbm, rot_ref, out_ref,
    G, T, acc, RO, RI, OS, IS,
    load_sem, own_sem, g_recv, g_send,
    ro_recv, ro_send, ri_recv, ri_send,
    os_recv, os_send, osr_send, is_sem,
):
    z, x, h = lax.axis_index("dp"), lax.axis_index("ctx"), lax.axis_index("hidden")
    nc = n_out + n_in
    nb = nc - n_a
    w = bi_hbm.shape[0]
    d_out = grad_hbm.shape[1]
    d_in = act_hbm.shape[1]
    z_last = jnp.where(z < 2, NZ - 1, 0)

    def rows(xx):
        return pl.ds(pl.multiple_of(xx * w, w), w)

    def lanes(c):
        return pl.ds(pl.multiple_of(c * CHUNK, CHUNK), CHUNK)

    own_in = pltpu.make_async_copy(
        bi_hbm, G.at[z, rows(x), pl.ds(d_out, d_in)], own_sem.at[0])
    own_out = pltpu.make_async_copy(
        bo_hbm, G.at[z, rows(x), pl.ds(0, d_out)], own_sem.at[1])
    own_out.start()
    own_in.start()

    barrier = pltpu.get_barrier_semaphore()
    pl.semaphore_signal(barrier, inc=1, device_id={"ctx": 1 - x}, device_id_type=MESH)
    for k in range(1, NZ):
        pl.semaphore_signal(
            barrier, inc=1, device_id={"hidden": lax.rem(h + k, NZ)}, device_id_type=MESH)

    @pl.when(z > 0)
    def _():
        pl.semaphore_signal(barrier, inc=1, device_id={"dp": z - 1}, device_id_type=MESH)

    @pl.when(z < NZ - 1)
    def _():
        pl.semaphore_signal(barrier, inc=1, device_id={"dp": z + 1}, device_id_type=MESH)

    pl.semaphore_wait(
        barrier, NZ + jnp.where(z > 0, 1, 0) + jnp.where(z < NZ - 1, 1, 0))

    def piece(way, zs, xx, c):
        dev = ({"dp": z + 1}, {"dp": z - 1}, {"ctx": 1 - x})[way]
        ref = G.at[zs, rows(xx), lanes(c)]
        return pltpu.make_async_remote_copy(
            src_ref=ref, dst_ref=ref, send_sem=g_send.at[way, zs, xx],
            recv_sem=g_recv.at[zs, xx, c], device_id=dev, device_id_type=MESH)

    def bulk(way, zs, xx, first, count):
        dev = ({"dp": z + 1}, {"dp": z - 1}, {"ctx": 1 - x})[way]
        ref = G.at[zs, rows(xx), pl.ds(first * CHUNK, count * CHUNK)]
        return pltpu.make_async_remote_copy(
            src_ref=ref, dst_ref=ref, send_sem=g_send.at[way, zs, xx],
            recv_sem=g_recv.at[zs, xx, 0], device_id=dev, device_id_type=MESH)

    own_out.wait()
    own_in.wait()

    def first_sends(i, carry):
        @pl.when(z < NZ - 1)
        def _():
            piece(0, z, x, i).start()

        @pl.when(z > 0)
        def _():
            piece(1, z, x, i).start()

        piece(2, z, x, jnp.where(i < n_a, nb + i, i - n_a)).start()
        return carry

    lax.fori_loop(0, nc, first_sends, 0)

    load_out = pltpu.make_async_copy(grad_hbm, T.at[:, pl.ds(0, d_out)], load_sem.at[0])
    load_in = pltpu.make_async_copy(act_hbm, T.at[:, pl.ds(d_out, d_in)], load_sem.at[1])
    load_out.start()
    load_in.start()
    acc[...] = jnp.zeros_like(acc)
    load_out.wait()
    load_in.wait()

    def multiply(zs, c):
        side = jnp.where(c < n_out, 0, 1)
        acc[side, zs] += lax.dot_general(
            G[zs, :, lanes(c)], T[:, lanes(c)], NT, preferred_element_type=jnp.float32)

    per_round = nc + n_a

    def z_step(t):
        r, i = lax.div(t, per_round) + 1, lax.rem(t, per_round)
        c = jnp.where(i < nc, i, i - n_a)
        xx = jnp.where(i < nc, x, 1 - x)
        for up in (True, False):
            zs = z + r if up else z - r

            @pl.when((zs < NZ) if up else (zs >= 0))
            def _(zs=zs, up=up):
                piece(0, zs, xx, c).wait_recv()
                if up:
                    @pl.when(z > 0)
                    def _():
                        piece(1, zs, xx, c).start()
                else:
                    @pl.when(z < NZ - 1)
                    def _():
                        piece(0, zs, xx, c).start()

                @pl.when(i < nb)
                def _():
                    piece(2, zs, xx, c).start()

                @pl.when(i >= nc)
                def _():
                    multiply(zs, c)

    n_units = nc + (NZ - 1) * nb

    def unit(n):
        m = n - nc
        ends = (z == 0) | (z == NZ - 1)
        r = lax.div(m, nb) + 1
        z_end, c_end = jnp.where(z == 0, r, NZ - 1 - r), lax.rem(m, nb)
        near = m < 2 * nb
        z_mid = jnp.where(near, jnp.where(lax.rem(m, 2) == 0, z + 1, z - 1), z_last)
        c_mid = jnp.where(near, lax.div(m, 2), m - 2 * nb)
        own = n < nc
        zs = jnp.where(own, z, jnp.where(ends, z_end, z_mid))
        c = jnp.where(
            own, jnp.where(n < n_a, nb + n, n - n_a), jnp.where(ends, c_end, c_mid))
        return zs, c

    def x_step(n):
        zs, c = unit(n)
        piece(2, zs, 1 - x, c).wait_recv()

        @pl.when(n < n_a)
        def _():
            @pl.when(z < NZ - 1)
            def _():
                piece(0, z, 1 - x, c).start()

            @pl.when(z > 0)
            def _():
                piece(1, z, 1 - x, c).start()

        multiply(zs, c)

    def part(side, to, frm):
        buf, ssem, rsem = ((RO, ro_send, ro_recv), (RI, ri_send, ri_recv))[side]
        return pltpu.make_async_remote_copy(
            src_ref=acc.at[side, to], dst_ref=buf.at[frm], send_sem=ssem.at[to],
            recv_sem=rsem.at[frm], device_id={"hidden": to}, device_id_type=MESH)

    def send_parts(side, last):
        for to in range(NZ):
            @pl.when((h != to) & ((z_last == to) if last else (z_last != to)))
            def _(to=to):
                part(side, to, h).start()

    def summed(side):
        buf = RI if side else RO
        value = acc[side, h]
        for k in range(1, NZ):
            frm = lax.rem(h + k, NZ)
            part(side, h, frm).wait_recv()
            value = value + buf[frm]
        return value.astype(jnp.bfloat16)

    blk = acc.shape[2]

    def block_of(hh):
        return pl.ds(pl.multiple_of(hh * blk, blk), blk)

    def os_copy(xx, hh, dev, sem):
        ref = OS.at[xx, block_of(hh), :]
        return pltpu.make_async_remote_copy(
            src_ref=ref, dst_ref=ref, send_sem=sem, recv_sem=os_recv.at[xx, hh],
            device_id=dev, device_id_type=MESH)

    def is_copy(xx):
        return pltpu.make_async_remote_copy(
            src_ref=IS.at[xx], dst_ref=IS.at[xx], send_sem=is_sem.at[0],
            recv_sem=is_sem.at[1], device_id={"ctx": 1 - x}, device_id_type=MESH)

    def finish_in():
        IS[x] = summed(1)
        is_copy(x).start()

    out_early = nc + 2 * nb - (nb - n_out)
    in_early = nc + 2 * nb
    out_late = nc + 2 * nb + n_out
    step_1 = out_late + 4
    step_2 = step_1 + 3

    def stages(n):
        @pl.when(n == out_early)
        def _():
            send_parts(0, False)

        @pl.when(n == in_early)
        def _():
            send_parts(1, False)

        @pl.when(n == out_late)
        def _():
            send_parts(0, True)

        @pl.when(n == step_1)
        def _():
            OS[x, block_of(h), :] = summed(0)
            os_copy(x, h, {"ctx": 1 - x}, os_send.at[0]).start()
            for k in range(1, NZ):
                os_copy(x, h, {"hidden": lax.rem(h + k, NZ)}, os_send.at[k]).start()

            @pl.when(h != z_last)
            def _():
                finish_in()

        @pl.when(n == step_2)
        def _():
            os_copy(1 - x, h, {"ctx": 1 - x}, os_send.at[0]).wait_recv()
            for k in range(1, NZ):
                os_copy(1 - x, h, {"hidden": lax.rem(h + k, NZ)}, osr_send.at[k - 1]).start()

    n_z = per_round * (NZ - 1)

    def body(t, carry):
        @pl.when(t < n_z)
        def _():
            z_step(t)

        n = t - LAG

        @pl.when((n >= 0) & (n < n_units))
        def _():
            x_step(n)

        stages(n)
        return carry

    lax.fori_loop(0, max(n_z, n_units + LAG), body, 0)

    send_parts(1, True)

    @pl.when(h == z_last)
    def _():
        finish_in()

    for k in range(1, NZ):
        for xx in range(2):
            os_copy(xx, lax.rem(h + k, NZ), {"ctx": 1 - x}, os_send.at[0]).wait_recv()

    total = lax.dot_general(OS[x], IS[x], NT, preferred_element_type=jnp.float32)
    is_copy(1 - x).wait_recv()
    total = total + lax.dot_general(OS[1 - x], IS[1 - x], NT, preferred_element_type=jnp.float32)
    out_ref[...] = jnp.dot(
        rot_ref[...], total.astype(jnp.bfloat16), preferred_element_type=jnp.float32)

    is_copy(x).wait_send()
    for k in range(NZ):
        os_copy(x, h, {"ctx": 1 - x}, os_send.at[k]).wait_send()
        if k:
            os_copy(x, h, {"ctx": 1 - x}, osr_send.at[k - 1]).wait_send()
    for to in range(NZ):
        @pl.when(h != to)
        def _(to=to):
            part(0, to, h).wait_send()
            part(1, to, h).wait_send()
    for zs in range(NZ):
        for way, sends in ((0, (z < NZ - 1) & (zs <= z)), (1, (z > 0) & (zs >= z))):
            @pl.when(sends)
            def _(way=way, zs=zs):
                bulk(way, zs, x, 0, nc).wait_send()
                bulk(way, zs, 1 - x, nb, n_a).wait_send()

        @pl.when(zs == z)
        def _(zs=zs):
            bulk(2, zs, x, 0, nc).wait_send()

        @pl.when(zs != z)
        def _(zs=zs):
            bulk(2, zs, x, 0, nb).wait_send()


def fast(activations, out_grads, input_basis, output_basis, rotation):
    tokens = activations.reshape(-1, activations.shape[-1])
    grad_rows = out_grads.reshape(-1, out_grads.shape[-1])
    d_in, d_out = tokens.shape[1], grad_rows.shape[1]
    width = d_in + d_out
    m = tokens.shape[0]
    w = input_basis.shape[1]
    rank = rotation.shape[1]
    blk = 2 * w
    n_out, n_in = d_out // CHUNK, d_in // CHUNK
    nc = n_out + n_in
    n_a = max(1, round(0.18 * nc))
    dma = pltpu.SemaphoreType.DMA
    f32, bf16 = jnp.float32, jnp.bfloat16
    anym = pl.BlockSpec(memory_space=pl.ANY)
    vmem = pl.BlockSpec(memory_space=pltpu.VMEM)
    logged = pl.pallas_call(
        functools.partial(kernel, n_out, n_in, n_a),
        out_shape=jax.ShapeDtypeStruct((rotation.shape[0], blk), f32),
        in_specs=[anym, anym, anym, anym, vmem],
        out_specs=vmem,
        scratch_shapes=[
            pltpu.VMEM((NZ, blk, width), bf16),
            pltpu.VMEM((m, width), bf16),
            pltpu.VMEM((2, NZ, blk, m), f32),
            pltpu.VMEM((NZ, blk, m), f32),
            pltpu.VMEM((NZ, blk, m), f32),
            pltpu.VMEM((2, rank, m), bf16),
            pltpu.VMEM((2, blk, m), bf16),
            dma((2,)), dma((2,)), dma((NZ, 2, nc)), dma((3, NZ, 2)),
            dma((NZ,)), dma((NZ,)), dma((NZ,)), dma((NZ,)),
            dma((2, NZ)), dma((NZ,)), dma((NZ,)), dma((2,)),
        ],
        compiler_params=pltpu.CompilerParams(
            collective_id=0, has_side_effects=True, vmem_limit_bytes=60 * 2**20),
    )(tokens, grad_rows, input_basis.T, output_basis.T, rotation)
    return logged.reshape(1, logged.shape[0], logged.shape[1])


def solution(mesh):
    size = mesh.shape

    def program(activations, out_grads, input_basis, output_basis, rotation):
        fits = (
            size["dp"] == NZ and size["hidden"] == NZ and size["ctx"] == 2
            and activations.shape[2] % (CHUNK * size["hidden"]) == 0
            and out_grads.shape[2] % (CHUNK * size["hidden"]) == 0
        )
        return jax.shard_map(
            fast if fits else local,
            mesh=mesh,
            in_specs=(
                P("dp", "ctx", "hidden"),
                P("dp", "ctx", "hidden"),
                P("hidden", ("dp", "ctx")),
                P("hidden", ("dp", "ctx")),
                P("ctx", None),
            ),
            out_specs=P("dp", "ctx", "hidden"),
            check_vma=False,
        )(activations, out_grads, input_basis, output_basis, rotation)

    return program
```

```python
import jax
import jax.numpy as jnp
from jax import lax
from jax.experimental import pallas as pl
from jax.experimental.pallas import tpu as pltpu
from jax.sharding import PartitionSpec as P

MESH = pl.DeviceIdType.MESH
NT = (((1,), (1,)), ((), ()))
NZ = 4
NC = 17
M0 = 9
N_M = 3
K0 = 12
N_K = 3
A0 = 15
N_A = 2
N_W = N_M + N_K
N_B = K0
N_E = NC - N_K
OUT_AT = 8
N_OUT = 4
LAG = 1
DELAY = 18
PAUSE, HOLD = 35, 4
OUT_EARLY, HELP, OUT_LATE, OTHER_A, OUT_SUM, IN_EARLY, OUT_RELAY = 34, 42, 43, 45, 47, 48, 50


def outer_sum(left, right):
    return lax.dot_general(
        left, right, (((0,), (0,)), ((), ())), preferred_element_type=jnp.float32
    )


def local(activations, out_grads, input_basis, output_basis, rotation):
    tokens = activations.reshape(-1, activations.shape[-1])
    grad_rows = out_grads.reshape(-1, out_grads.shape[-1])
    in_part = jnp.dot(
        tokens,
        lax.all_gather(input_basis, ("dp", "ctx"), axis=1, tiled=True),
        preferred_element_type=jnp.float32,
    )
    out_part = jnp.dot(
        grad_rows,
        lax.all_gather(output_basis, ("dp", "ctx"), axis=1, tiled=True),
        preferred_element_type=jnp.float32,
    )
    in_cols = lax.psum_scatter(in_part, "hidden", scatter_dimension=1, tiled=True).astype(
        jnp.bfloat16
    )
    out_side = lax.psum(out_part, "hidden")
    out_side = out_side.astype(jnp.bfloat16)
    total = lax.psum(outer_sum(out_side, in_cols), "ctx")
    lowrank = total.astype(jnp.bfloat16)
    logged = jnp.dot(rotation, lowrank, preferred_element_type=jnp.float32)
    return logged.reshape(1, logged.shape[0], logged.shape[1])


def kernel(
    act_hbm, grad_hbm, bi_hbm, bo_hbm, rot_ref, out_ref,
    G, T, acc, RO, RI, OS, IS, TN, PA, PS, PR,
    load_sem, own_sem, g_recv, g_send,
    ro_recv, ro_send, ri_recv, ri_send,
    os_recv, os_send, osr_send, is_sem,
    t_recv, t_send, p_recv, p_send,
):
    z, x, h = lax.axis_index("dp"), lax.axis_index("ctx"), lax.axis_index("hidden")
    chunk = G.shape[2] // NC
    w = bi_hbm.shape[0]
    d_out = grad_hbm.shape[1]
    d_in = act_hbm.shape[1]
    head = OUT_AT * chunk
    low = z < 2
    end = (z == 0) | (z == NZ - 1)
    mid = jnp.logical_not(end)
    z_last = jnp.where(low, NZ - 1, 0)
    inward = jnp.where(low, z + 1, z - 1)
    outward = jnp.where(low, 0, NZ - 1)
    far = z_last

    def rows(xx):
        return pl.ds(pl.multiple_of(xx * w, w), w)

    def lanes(c):
        return pl.ds(pl.multiple_of(c * chunk, chunk), chunk)

    def local_parts(src_in, src_out, dst, sem):
        return (
            pltpu.make_async_copy(src_out, dst(head, d_out), sem.at[0]),
            pltpu.make_async_copy(src_in.at[:, pl.ds(0, head)], dst(0, head), sem.at[1]),
            pltpu.make_async_copy(
                src_in.at[:, pl.ds(head, d_in - head)],
                dst(head + d_out, d_in - head), sem.at[2]),
        )

    own = local_parts(
        bi_hbm, bo_hbm, lambda a, n: G.at[z, rows(x), pl.ds(a, n)], own_sem)
    load = local_parts(act_hbm, grad_hbm, lambda a, n: T.at[:, pl.ds(a, n)], load_sem)
    for copy in own:
        copy.start()

    barrier = pltpu.get_barrier_semaphore()
    pl.semaphore_signal(barrier, inc=1, device_id={"ctx": 1 - x}, device_id_type=MESH)
    pl.semaphore_signal(barrier, inc=1, device_id={"dp": inward}, device_id_type=MESH)
    for k in range(1, NZ):
        pl.semaphore_signal(
            barrier, inc=1, device_id={"hidden": lax.rem(h + k, NZ)}, device_id_type=MESH)

    @pl.when(mid)
    def _():
        pl.semaphore_signal(barrier, inc=1, device_id={"dp": outward}, device_id_type=MESH)

    pl.semaphore_wait(barrier, NZ + 1 + jnp.where(mid, 1, 0))

    def device(way):
        return ({"dp": inward}, {"dp": outward}, {"ctx": 1 - x})[way]

    def piece(way, zs, xx, c):
        ref = G.at[zs, rows(xx), lanes(c)]
        return pltpu.make_async_remote_copy(
            src_ref=ref, dst_ref=ref, send_sem=g_send.at[way, zs, xx],
            recv_sem=g_recv.at[zs, xx, c], device_id=device(way), device_id_type=MESH)

    def sent(way, zs, xx, first, stop):
        ref = G.at[zs, rows(xx), pl.ds(first * chunk, (stop - first) * chunk)]
        pltpu.make_async_remote_copy(
            src_ref=ref, dst_ref=ref, send_sem=g_send.at[way, zs, xx],
            recv_sem=g_recv.at[zs, xx, 0], device_id=device(way), device_id_type=MESH,
        ).wait_send()

    def arrived(zs, xx, c):
        piece(2, zs, xx, c).wait_recv()

    def plain(i):
        return jnp.where(i == 0, OUT_AT, i - 1)

    def order_all(i):
        return jnp.where(
            i < N_K, K0 + i,
            jnp.where(i < N_K + N_M, M0 + i - N_K,
                      jnp.where(i < A0, plain(i - N_K - N_M), i)))

    def order_kept(i):
        return order_all(i + N_K)

    for copy in own:
        copy.wait()
    for copy in load:
        copy.start()

    def first_sends(i, carry):
        piece(0, z, x, order_all(i)).start()

        @pl.when(mid)
        def _():
            @pl.when(i < N_E)
            def _():
                piece(1, z, x, order_kept(i)).start()

            piece(2, z, x, jnp.where(i < N_A, A0 + i, order_all(i - N_A))).start()

        @pl.when(end & (i < N_E))
        def _():
            piece(2, z, x, jnp.where(i < N_A, A0 + i, order_kept(i - N_A))).start()

        return carry

    lax.fori_loop(0, NC, first_sends, 0)

    def t_copy(k):
        return pltpu.make_async_remote_copy(
            src_ref=T.at[:, pl.ds((K0 + k) * chunk, chunk)],
            dst_ref=TN.at[:, pl.ds(k * chunk, chunk)],
            send_sem=t_send.at[k], recv_sem=t_recv.at[k],
            device_id=device(0), device_id_type=MESH)

    acc[...] = jnp.zeros_like(acc)
    for copy in load:
        copy.wait()

    @pl.when(end)
    def _():
        for k in range(N_K):
            t_copy(k).start()

    def multiply(zs, c):
        side = jnp.where((c >= OUT_AT) & (c < OUT_AT + N_OUT), 0, 1)
        acc[side, zs] += lax.dot_general(
            G[zs, :, lanes(c)], T[:, lanes(c)], NT, preferred_element_type=jnp.float32)

    per_round = N_E + N_A

    def end_z(t):
        tt = jnp.where(t < PAUSE, t, t - HOLD)
        r, i = lax.div(tt, per_round) + 1, lax.rem(tt, per_round)
        zs = jnp.where(low, r, NZ - 1 - r)
        from_own = i < N_E
        c = jnp.where(from_own, order_kept(i), A0 + i - N_E)
        xx = jnp.where(from_own, x, 1 - x)
        arrived(zs, xx, c)

        @pl.when(i < N_B)
        def _():
            piece(2, zs, xx, c).start()

        @pl.when(i >= N_E)
        def _():
            multiply(zs, c)

    def mid_outer(t):
        @pl.when(t < NC)
        def _():
            c = order_all(t)
            arrived(outward, x, c)

            @pl.when(t < N_W)
            def _():
                piece(0, outward, x, c).start()

            @pl.when(t < A0)
            def _():
                piece(2, outward, x, c).start()

        @pl.when((t >= N_W + DELAY) & (t < NC + DELAY))
        def _():
            piece(0, outward, x, order_all(t - DELAY)).start()

        @pl.when((t >= OTHER_A) & (t < OTHER_A + N_A))
        def _():
            c = A0 + t - OTHER_A
            arrived(outward, 1 - x, c)
            piece(0, outward, 1 - x, c).start()
            multiply(outward, c)

    def mid_across(t):
        s = t - NC
        mixed = 2 * (N_W + N_A)
        near = t < NC
        i_far = jnp.where(
            s < mixed - 2 * N_A, lax.div(s, 2), s - (N_W + N_A) - N_W)
        is_near_other = (s >= 0) & (
            ((s < 2 * N_W) & (lax.rem(s, 2) == 1))
            | ((s >= 2 * N_W) & (s < 2 * N_W + N_A)))
        o = jnp.where(s < 2 * N_W, lax.div(s, 2), s - N_W)
        c_other = jnp.where(o < N_A, A0 + o, order_all(o - N_A))
        u = s - (2 * N_W + N_A)
        far_w = (u >= 0) & (u < N_W)
        far_a = u >= N_W + NC - N_W
        far_other = far_w | far_a
        c_far_other = jnp.where(far_w, order_all(u), A0 + u - NC)
        c = jnp.where(
            near, order_all(t),
            jnp.where(is_near_other, c_other,
                      jnp.where(far_other, c_far_other, order_all(i_far))))
        zs = jnp.where(near | is_near_other, inward, far)
        other = is_near_other | far_other
        xx = jnp.where(other, 1 - x, x)
        arrived(zs, xx, c)
        crossing = c >= A0

        @pl.when(crossing | (jnp.logical_not(other) & (c < K0)))
        def _():
            piece(1, zs, xx, c).start()

        @pl.when(jnp.logical_not(other) & (c < M0))
        def _():
            piece(2, zs, xx, c).start()

        @pl.when(other)
        def _():
            multiply(zs, c)

    def x_step(n):
        m = n - N_E
        r = lax.div(m, N_B) + 1
        own_e = n < N_E
        z_e = jnp.where(own_e, z, jnp.where(low, r, NZ - 1 - r))
        c_e = jnp.where(
            own_e, jnp.where(n < N_A, A0 + n, order_kept(n - N_A)), order_kept(lax.rem(m, N_B)))
        m = n - NC
        v = m - N_W
        own_m = n < NC
        first = m < N_W
        pair = v < 2 * M0
        even = first | (pair & (lax.rem(v, 2) == 0))
        z_m = jnp.where(
            own_m, z, jnp.where(even, outward, jnp.where(pair, inward, far)))
        c_m = jnp.where(
            own_m, jnp.where(n < N_A, A0 + n, order_all(n - N_A)),
            jnp.where(first, order_all(m),
                      jnp.where(pair, plain(lax.div(v, 2)), plain(v - 2 * M0))))
        zs, c = jnp.where(end, z_e, z_m), jnp.where(end, c_e, c_m)
        arrived(zs, 1 - x, c)

        @pl.when((n < N_A) | (mid & (n < N_A + N_W)) | (mid & (n >= NC) & (n < NC + N_W)))
        def _():
            piece(0, zs, 1 - x, c).start()

        @pl.when(mid & (n < N_A))
        def _():
            piece(1, zs, 1 - x, c).start()

        multiply(zs, c)

    def p_copy(zs):
        return pltpu.make_async_remote_copy(
            src_ref=PS.at[zs], dst_ref=PR.at[zs], send_sem=p_send.at[zs],
            recv_sem=p_recv.at[zs], device_id=device(1), device_id_type=MESH)

    def help_end(zs):
        PA[...] = jnp.zeros_like(PA)

        def add(k, carry):
            PA[...] += lax.dot_general(
                G[zs, :, lanes(K0 + k)], TN[:, lanes(k)], NT,
                preferred_element_type=jnp.float32)
            return carry

        lax.fori_loop(0, N_K, add, 0)
        PS[zs] = PA[...].astype(jnp.bfloat16)
        p_copy(zs).start()

    def part(side, to, frm):
        buf, ssem, rsem = ((RO, ro_send, ro_recv), (RI, ri_send, ri_recv))[side]
        return pltpu.make_async_remote_copy(
            src_ref=acc.at[side, to], dst_ref=buf.at[frm], send_sem=ssem.at[to],
            recv_sem=rsem.at[frm], device_id={"hidden": to}, device_id_type=MESH)

    def send_parts(side, last):
        for to in range(NZ):
            @pl.when((h != to) & ((z_last == to) if last else (z_last != to)))
            def _(to=to):
                part(side, to, h).start()

    def summed(side):
        buf = RI if side else RO
        value = acc[side, h]
        for k in range(1, NZ):
            frm = lax.rem(h + k, NZ)
            part(side, h, frm).wait_recv()
            value = value + buf[frm]
        return value.astype(jnp.bfloat16)

    blk = acc.shape[2]

    def block_of(hh):
        return pl.ds(pl.multiple_of(hh * blk, blk), blk)

    def os_copy(xx, hh, dev, sem):
        ref = OS.at[xx, block_of(hh), :]
        return pltpu.make_async_remote_copy(
            src_ref=ref, dst_ref=ref, send_sem=sem, recv_sem=os_recv.at[xx, hh],
            device_id=dev, device_id_type=MESH)

    def is_copy(xx):
        return pltpu.make_async_remote_copy(
            src_ref=IS.at[xx], dst_ref=IS.at[xx], send_sem=is_sem.at[0],
            recv_sem=is_sem.at[1], device_id={"ctx": 1 - x}, device_id_type=MESH)

    def stages(t):
        @pl.when(t == OUT_EARLY)
        def _():
            send_parts(0, False)

        @pl.when(t == OUT_LATE)
        def _():
            send_parts(0, True)

        @pl.when(mid & (t == HELP))
        def _():
            for k in range(N_K):
                t_copy(k).wait_recv()

        @pl.when(mid & (t >= HELP) & (t < HELP + NZ))
        def _():
            k = t - HELP
            help_end(jnp.where(low, k, NZ - 1 - k))

        @pl.when(t == OUT_SUM)
        def _():
            OS[x, block_of(h), :] = summed(0)
            os_copy(x, h, {"ctx": 1 - x}, os_send.at[0]).start()
            for k in range(1, NZ):
                os_copy(x, h, {"hidden": lax.rem(h + k, NZ)}, os_send.at[k]).start()

        @pl.when(t == IN_EARLY)
        def _():
            @pl.when(end)
            def _():
                for zs in range(NZ):
                    p_copy(zs).wait_recv()
                    acc[1, zs] += PR[zs].astype(jnp.float32)

            send_parts(1, False)

        @pl.when(t == OUT_RELAY)
        def _():
            os_copy(1 - x, h, {"ctx": 1 - x}, os_send.at[0]).wait_recv()
            for k in range(1, NZ):
                os_copy(1 - x, h, {"hidden": lax.rem(h + k, NZ)}, osr_send.at[k - 1]).start()

    n_end = per_round * (NZ - 1)
    n_across = 2 * (NC + N_W + N_A)
    units_e, units_m = N_E + (NZ - 1) * N_B, NC + N_W + 3 * M0

    def body(t, carry):
        @pl.when(end & ((t < PAUSE) | ((t >= PAUSE + HOLD) & (t < n_end + HOLD))))
        def _():
            end_z(t)

        @pl.when(mid)
        def _():
            mid_outer(t)

            @pl.when(t < n_across)
            def _():
                mid_across(t)

        n = t - LAG

        @pl.when((n >= 0) & (n < jnp.where(end, units_e, units_m)))
        def _():
            x_step(n)

        stages(t)
        return carry

    lax.fori_loop(0, max(n_end + HOLD, n_across, units_e + LAG, units_m + LAG), body, 0)

    send_parts(1, True)
    IS[x] = summed(1)
    is_copy(x).start()

    for k in range(1, NZ):
        for xx in range(2):
            os_copy(xx, lax.rem(h + k, NZ), {"ctx": 1 - x}, os_send.at[0]).wait_recv()

    total = lax.dot_general(OS[x], IS[x], NT, preferred_element_type=jnp.float32)
    is_copy(1 - x).wait_recv()
    total = total + lax.dot_general(OS[1 - x], IS[1 - x], NT, preferred_element_type=jnp.float32)
    out_ref[...] = jnp.dot(
        rot_ref[...], total.astype(jnp.bfloat16), preferred_element_type=jnp.float32)

    is_copy(x).wait_send()
    for k in range(NZ):
        os_copy(x, h, {"ctx": 1 - x}, os_send.at[k]).wait_send()
        if k:
            os_copy(x, h, {"ctx": 1 - x}, osr_send.at[k - 1]).wait_send()
    for to in range(NZ):
        @pl.when(h != to)
        def _(to=to):
            part(0, to, h).wait_send()
            part(1, to, h).wait_send()

    @pl.when(end)
    def _():
        sent(0, z, x, 0, NC)
        sent(0, z, 1 - x, A0, NC)
        for k in range(N_K):
            t_copy(k).wait_send()
        sent(2, z, x, 0, K0)
        sent(2, z, x, A0, NC)
        for r in range(1, NZ):
            sent(2, jnp.where(low, r, NZ - 1 - r), x, 0, K0)

    @pl.when(mid)
    def _():
        for zs in (z, outward):
            sent(0, zs, x, 0, NC)
            sent(0, zs, 1 - x, M0, NC)
        for zs in (z, inward, far):
            sent(1, zs, x, 0, K0)
            sent(1, zs, x, A0, NC)
            sent(1, zs, 1 - x, A0, NC)
        sent(2, z, x, 0, NC)
        sent(2, outward, x, 0, A0)
        sent(2, inward, x, 0, M0)
        sent(2, far, x, 0, M0)
        for zs in range(NZ):
            p_copy(zs).wait_send()


def fast(activations, out_grads, input_basis, output_basis, rotation):
    tokens = activations.reshape(-1, activations.shape[-1])
    grad_rows = out_grads.reshape(-1, out_grads.shape[-1])
    d_in, d_out = tokens.shape[1], grad_rows.shape[1]
    width = d_in + d_out
    m = tokens.shape[0]
    w = input_basis.shape[1]
    rank = rotation.shape[1]
    blk = 2 * w
    dma = pltpu.SemaphoreType.DMA
    f32, bf16 = jnp.float32, jnp.bfloat16
    anym = pl.BlockSpec(memory_space=pl.ANY)
    vmem = pl.BlockSpec(memory_space=pltpu.VMEM)
    logged = pl.pallas_call(
        kernel,
        out_shape=jax.ShapeDtypeStruct((rotation.shape[0], blk), f32),
        in_specs=[anym, anym, anym, anym, vmem],
        out_specs=vmem,
        scratch_shapes=[
            pltpu.VMEM((NZ, blk, width), bf16),
            pltpu.VMEM((m, width), bf16),
            pltpu.VMEM((2, NZ, blk, m), f32),
            pltpu.VMEM((NZ, blk, m), f32),
            pltpu.VMEM((NZ, blk, m), f32),
            pltpu.VMEM((2, rank, m), bf16),
            pltpu.VMEM((2, blk, m), bf16),
            pltpu.VMEM((m, width // NC * N_K), bf16),
            pltpu.VMEM((blk, m), f32),
            pltpu.VMEM((NZ, blk, m), bf16),
            pltpu.VMEM((NZ, blk, m), bf16),
            dma((3,)), dma((3,)), dma((NZ, 2, NC)), dma((3, NZ, 2)),
            dma((NZ,)), dma((NZ,)), dma((NZ,)), dma((NZ,)),
            dma((2, NZ)), dma((NZ,)), dma((NZ,)), dma((2,)),
            dma((N_K,)), dma((N_K,)), dma((NZ,)), dma((NZ,)),
        ],
        compiler_params=pltpu.CompilerParams(
            collective_id=0, has_side_effects=True, vmem_limit_bytes=60 * 2**20),
    )(tokens, grad_rows, input_basis.T, output_basis.T, rotation)
    return logged.reshape(1, logged.shape[0], logged.shape[1])


def solution(mesh):
    size = mesh.shape

    def program(activations, out_grads, input_basis, output_basis, rotation):
        fits = (
            size["dp"] == NZ and size["hidden"] == NZ and size["ctx"] == 2
            and out_grads.shape[2] % (128 * N_OUT * NZ) == 0
            and activations.shape[2] * N_OUT == out_grads.shape[2] * (NC - N_OUT)
        )
        return jax.shard_map(
            fast if fits else local,
            mesh=mesh,
            in_specs=(
                P("dp", "ctx", "hidden"),
                P("dp", "ctx", "hidden"),
                P("hidden", ("dp", "ctx")),
                P("hidden", ("dp", "ctx")),
                P("ctx", None),
            ),
            out_specs=P("dp", "ctx", "hidden"),
            check_vma=False,
        )(activations, out_grads, input_basis, output_basis, rotation)

    return program
```

```python
import jax
import jax.numpy as jnp
from jax import lax
from jax.experimental import pallas as pl
from jax.experimental.pallas import tpu as pltpu
from jax.sharding import PartitionSpec as P

MESH = pl.DeviceIdType.MESH
NT = (((1,), (1,)), ((), ()))
NZ = 4
NC = 17
M0 = 9
N_M = 3
K0 = 12
N_K = 3
A0 = 15
N_A = 2
N_W = N_M + N_K
N_B = K0
N_E = NC - N_K
OUT_AT = 8
N_OUT = 4
LAG = 1
DELAY = 18
PAUSE, HOLD = 35, 4
MOVE, IN_FIRST, OUT_EARLY, OTHER_A, IN_SECOND = N_A + LAG, 28, 34, 35, 42
HELP, OUT_LATE, OUT_SUM, HELP_SUM, OUT_RELAY = 43, 43, 47, 50, 50


def outer_sum(left, right):
    return lax.dot_general(
        left, right, (((0,), (0,)), ((), ())), preferred_element_type=jnp.float32
    )


def local(activations, out_grads, input_basis, output_basis, rotation):
    tokens = activations.reshape(-1, activations.shape[-1])
    grad_rows = out_grads.reshape(-1, out_grads.shape[-1])
    in_part = jnp.dot(
        tokens,
        lax.all_gather(input_basis, ("dp", "ctx"), axis=1, tiled=True),
        preferred_element_type=jnp.float32,
    )
    out_part = jnp.dot(
        grad_rows,
        lax.all_gather(output_basis, ("dp", "ctx"), axis=1, tiled=True),
        preferred_element_type=jnp.float32,
    )
    in_cols = lax.psum_scatter(in_part, "hidden", scatter_dimension=1, tiled=True).astype(
        jnp.bfloat16
    )
    out_side = lax.psum(out_part, "hidden")
    out_side = out_side.astype(jnp.bfloat16)
    total = lax.psum(outer_sum(out_side, in_cols), "ctx")
    lowrank = total.astype(jnp.bfloat16)
    logged = jnp.dot(rotation, lowrank, preferred_element_type=jnp.float32)
    return logged.reshape(1, logged.shape[0], logged.shape[1])


def kernel(
    act_hbm, grad_hbm, bi_hbm, bo_hbm, rot_ref, out_ref,
    G, T, acc, RO, RI, OS, IS, TN, PA, PS, PQ, PT, PR,
    load_sem, own_sem, g_recv, g_send,
    ro_recv, ro_send, ri_recv, ri_send,
    os_recv, os_send, osr_send, is_sem,
    t_recv, t_send, p_recv, p_send, pt_sem,
):
    z, x, h = lax.axis_index("dp"), lax.axis_index("ctx"), lax.axis_index("hidden")
    chunk = G.shape[2] // NC
    w = bi_hbm.shape[0]
    d_out = grad_hbm.shape[1]
    d_in = act_hbm.shape[1]
    head = OUT_AT * chunk
    low = z < 2
    end = (z == 0) | (z == NZ - 1)
    mid = jnp.logical_not(end)
    z_last = jnp.where(low, NZ - 1, 0)
    inward = jnp.where(low, z + 1, z - 1)
    outward = jnp.where(low, 0, NZ - 1)
    far = z_last

    def rows(xx):
        return pl.ds(pl.multiple_of(xx * w, w), w)

    def lanes(c):
        return pl.ds(pl.multiple_of(c * chunk, chunk), chunk)

    def local_parts(src_in, src_out, dst, sem):
        return (
            pltpu.make_async_copy(src_out, dst(head, d_out), sem.at[0]),
            pltpu.make_async_copy(src_in.at[:, pl.ds(0, head)], dst(0, head), sem.at[1]),
            pltpu.make_async_copy(
                src_in.at[:, pl.ds(head, d_in - head)],
                dst(head + d_out, d_in - head), sem.at[2]),
        )

    own = local_parts(
        bi_hbm, bo_hbm, lambda a, n: G.at[z, rows(x), pl.ds(a, n)], own_sem)
    load = local_parts(act_hbm, grad_hbm, lambda a, n: T.at[:, pl.ds(a, n)], load_sem)
    for copy in own:
        copy.start()

    barrier = pltpu.get_barrier_semaphore()
    pl.semaphore_signal(barrier, inc=1, device_id={"ctx": 1 - x}, device_id_type=MESH)
    pl.semaphore_signal(barrier, inc=1, device_id={"dp": inward}, device_id_type=MESH)
    for k in range(1, NZ):
        pl.semaphore_signal(
            barrier, inc=1, device_id={"hidden": lax.rem(h + k, NZ)}, device_id_type=MESH)

    @pl.when(mid)
    def _():
        pl.semaphore_signal(barrier, inc=1, device_id={"dp": outward}, device_id_type=MESH)

    pl.semaphore_wait(barrier, NZ + 1 + jnp.where(mid, 1, 0))

    def device(way):
        return ({"dp": inward}, {"dp": outward}, {"ctx": 1 - x})[way]

    def piece(way, zs, xx, c):
        ref = G.at[zs, rows(xx), lanes(c)]
        return pltpu.make_async_remote_copy(
            src_ref=ref, dst_ref=ref, send_sem=g_send.at[way, zs, xx],
            recv_sem=g_recv.at[zs, xx, c], device_id=device(way), device_id_type=MESH)

    def sent(way, zs, xx, first, stop):
        ref = G.at[zs, rows(xx), pl.ds(first * chunk, (stop - first) * chunk)]
        pltpu.make_async_remote_copy(
            src_ref=ref, dst_ref=ref, send_sem=g_send.at[way, zs, xx],
            recv_sem=g_recv.at[zs, xx, 0], device_id=device(way), device_id_type=MESH,
        ).wait_send()

    def arrived(zs, xx, c):
        piece(2, zs, xx, c).wait_recv()

    def plain(i):
        return jnp.where(i == 0, OUT_AT, i - 1)

    def order_all(i):
        return jnp.where(
            i < N_K, K0 + i,
            jnp.where(i < N_K + N_M, M0 + i - N_K,
                      jnp.where(i < A0, plain(i - N_K - N_M), i)))

    def order_kept(i):
        return order_all(i + N_K)

    for copy in own:
        copy.wait()
    for copy in load:
        copy.start()

    def first_sends(i, carry):
        piece(0, z, x, order_all(i)).start()

        @pl.when(mid)
        def _():
            @pl.when(i < N_E)
            def _():
                piece(1, z, x, order_kept(i)).start()

            piece(2, z, x, jnp.where(i < N_A, A0 + i, order_all(i - N_A))).start()

        @pl.when(end & (i < N_E))
        def _():
            piece(2, z, x, jnp.where(i < N_A, A0 + i, order_kept(i - N_A))).start()

        return carry

    lax.fori_loop(0, NC, first_sends, 0)

    def t_copy(k):
        return pltpu.make_async_remote_copy(
            src_ref=T.at[:, pl.ds((K0 + k) * chunk, chunk)],
            dst_ref=TN.at[:, pl.ds(k * chunk, chunk)],
            send_sem=t_send.at[k], recv_sem=t_recv.at[k],
            device_id=device(0), device_id_type=MESH)

    acc[...] = jnp.zeros_like(acc)
    for copy in load:
        copy.wait()

    def multiply(zs, c):
        side = jnp.where((c >= OUT_AT) & (c < OUT_AT + N_OUT), 0, 1)
        acc[side, zs] += lax.dot_general(
            G[zs, :, lanes(c)], T[:, lanes(c)], NT, preferred_element_type=jnp.float32)

    per_round = N_E + N_A

    def end_z(t):
        tt = jnp.where(t < PAUSE, t, t - HOLD)
        r, i = lax.div(tt, per_round) + 1, lax.rem(tt, per_round)
        zs = jnp.where(low, r, NZ - 1 - r)
        from_own = i < N_E
        c = jnp.where(from_own, order_kept(i), A0 + i - N_E)
        xx = jnp.where(from_own, x, 1 - x)
        arrived(zs, xx, c)

        @pl.when(i < N_B)
        def _():
            piece(2, zs, xx, c).start()

        @pl.when(i >= N_E)
        def _():
            multiply(zs, c)

    def mid_outer(t):
        @pl.when(t < NC)
        def _():
            c = order_all(t)
            arrived(outward, x, c)

            @pl.when(t < N_W)
            def _():
                piece(0, outward, x, c).start()

            @pl.when(t < A0)
            def _():
                piece(2, outward, x, c).start()

        @pl.when((t >= N_W + DELAY) & (t < NC + DELAY))
        def _():
            piece(0, outward, x, order_all(t - DELAY)).start()

        @pl.when((t >= OTHER_A) & (t < OTHER_A + N_A))
        def _():
            c = A0 + t - OTHER_A
            arrived(outward, 1 - x, c)
            piece(0, outward, 1 - x, c).start()
            multiply(outward, c)

    def mid_across(t):
        s = t - NC
        mixed = 2 * (N_W + N_A)
        near = t < NC
        i_far = jnp.where(
            s < mixed - 2 * N_A, lax.div(s, 2), s - (N_W + N_A) - N_W)
        is_near_other = (s >= 0) & (
            ((s < 2 * N_W) & (lax.rem(s, 2) == 1))
            | ((s >= 2 * N_W) & (s < 2 * N_W + N_A)))
        o = jnp.where(s < 2 * N_W, lax.div(s, 2), s - N_W)
        c_other = jnp.where(o < N_A, A0 + o, order_all(o - N_A))
        u = s - (2 * N_W + N_A)
        far_w = (u >= 0) & (u < N_W)
        far_a = u >= N_W + NC - N_W
        far_other = far_w | far_a
        c_far_other = jnp.where(far_w, order_all(u), A0 + u - NC)
        c = jnp.where(
            near, order_all(t),
            jnp.where(is_near_other, c_other,
                      jnp.where(far_other, c_far_other, order_all(i_far))))
        zs = jnp.where(near | is_near_other, inward, far)
        other = is_near_other | far_other
        xx = jnp.where(other, 1 - x, x)
        arrived(zs, xx, c)
        crossing = c >= A0

        @pl.when(crossing | (jnp.logical_not(other) & (c < K0)))
        def _():
            piece(1, zs, xx, c).start()

        @pl.when(jnp.logical_not(other) & (c < M0))
        def _():
            piece(2, zs, xx, c).start()

        @pl.when(other)
        def _():
            multiply(zs, c)

    def x_step(n):
        m = n - N_E
        r = lax.div(m, N_B) + 1
        own_e = n < N_E
        z_e = jnp.where(own_e, z, jnp.where(low, r, NZ - 1 - r))
        c_e = jnp.where(
            own_e, jnp.where(n < N_A, A0 + n, order_kept(n - N_A)), order_kept(lax.rem(m, N_B)))
        m = n - NC
        v = m - N_W
        own_m = n < NC
        first = m < N_W
        pair = v < 2 * M0
        even = first | (pair & (lax.rem(v, 2) == 0))
        z_m = jnp.where(
            own_m, z, jnp.where(even, outward, jnp.where(pair, inward, far)))
        c_m = jnp.where(
            own_m, jnp.where(n < N_A, A0 + n, order_all(n - N_A)),
            jnp.where(first, order_all(m),
                      jnp.where(pair, plain(lax.div(v, 2)), plain(v - 2 * M0))))
        zs, c = jnp.where(end, z_e, z_m), jnp.where(end, c_e, c_m)
        arrived(zs, 1 - x, c)

        @pl.when((n < N_A) | (mid & (n < N_A + N_W)) | (mid & (n >= NC) & (n < NC + N_W)))
        def _():
            piece(0, zs, 1 - x, c).start()

        @pl.when(mid & (n < N_A))
        def _():
            piece(1, zs, 1 - x, c).start()

        multiply(zs, c)

    def p_copy(to, frm):
        return pltpu.make_async_remote_copy(
            src_ref=PS.at[to], dst_ref=PQ.at[frm], send_sem=p_send.at[to],
            recv_sem=p_recv.at[frm], device_id={"hidden": to}, device_id_type=MESH)

    def pt_copy(way):
        return pltpu.make_async_remote_copy(
            src_ref=PT, dst_ref=PR, send_sem=pt_sem.at[0], recv_sem=pt_sem.at[1],
            device_id=device(way), device_id_type=MESH)

    def help_end(zs):
        PA[zs] = jnp.zeros_like(PA[zs])

        def add(k, carry):
            PA[zs] += lax.dot_general(
                G[zs, :, lanes(K0 + k)], TN[:, lanes(k)], NT,
                preferred_element_type=jnp.float32)
            return carry

        lax.fori_loop(0, N_K, add, 0)

        @pl.when(zs != h)
        def _():
            PS[zs] = PA[zs].astype(jnp.bfloat16)
            p_copy(zs, h).start()

    def help_sum():
        value = PA[h]
        for k in range(1, NZ):
            frm = lax.rem(h + k, NZ)
            p_copy(h, frm).wait_recv()
            value = value + PQ[frm].astype(jnp.float32)
        PT[...] = value.astype(jnp.bfloat16)
        pt_copy(1).start()

    def part(side, to, frm):
        buf, ssem, rsem = ((RO, ro_send, ro_recv), (RI, ri_send, ri_recv))[side]
        return pltpu.make_async_remote_copy(
            src_ref=acc.at[side, to], dst_ref=buf.at[frm], send_sem=ssem.at[to],
            recv_sem=rsem.at[frm], device_id={"hidden": to}, device_id_type=MESH)

    def send_parts(side, which):
        for to in range(NZ):
            @pl.when((h != to) & which(to))
            def _(to=to):
                part(side, to, h).start()

    def is_last(to):
        return z_last == to

    def not_last(to):
        return z_last != to

    def is_first(to):
        return (z == to) | (end & (inward == to))

    def is_second(to):
        return (z_last != to) & (z != to) & (mid | (inward != to))

    def summed(side):
        buf = RI if side else RO
        value = acc[side, h]
        for k in range(1, NZ):
            frm = lax.rem(h + k, NZ)
            part(side, h, frm).wait_recv()
            value = value + buf[frm]
        return value.astype(jnp.bfloat16)

    blk = acc.shape[2]

    def block_of(hh):
        return pl.ds(pl.multiple_of(hh * blk, blk), blk)

    def os_copy(xx, hh, dev, sem):
        ref = OS.at[xx, block_of(hh), :]
        return pltpu.make_async_remote_copy(
            src_ref=ref, dst_ref=ref, send_sem=sem, recv_sem=os_recv.at[xx, hh],
            device_id=dev, device_id_type=MESH)

    def is_copy(xx):
        return pltpu.make_async_remote_copy(
            src_ref=IS.at[xx], dst_ref=IS.at[xx], send_sem=is_sem.at[0],
            recv_sem=is_sem.at[1], device_id={"ctx": 1 - x}, device_id_type=MESH)

    def stages(t):
        @pl.when(end & (t == MOVE))
        def _():
            for k in range(N_K):
                t_copy(k).start()

        @pl.when(t == OUT_EARLY)
        def _():
            send_parts(0, not_last)

        @pl.when(t == OUT_LATE)
        def _():
            send_parts(0, is_last)

        @pl.when(mid & (t == HELP))
        def _():
            for k in range(N_K):
                t_copy(k).wait_recv()

        @pl.when(mid & (t >= HELP) & (t < HELP + NZ))
        def _():
            k = t - HELP
            help_end(jnp.where(low, k, NZ - 1 - k))

        @pl.when(t == OUT_SUM)
        def _():
            OS[x, block_of(h), :] = summed(0)
            os_copy(x, h, {"ctx": 1 - x}, os_send.at[0]).start()
            for k in range(1, NZ):
                os_copy(x, h, {"hidden": lax.rem(h + k, NZ)}, os_send.at[k]).start()

        @pl.when(t == IN_FIRST)
        def _():
            send_parts(1, is_first)

        @pl.when(t == IN_SECOND)
        def _():
            send_parts(1, is_second)

        @pl.when(mid & (t == HELP_SUM))
        def _():
            help_sum()

        @pl.when(t == OUT_RELAY)
        def _():
            os_copy(1 - x, h, {"ctx": 1 - x}, os_send.at[0]).wait_recv()
            for k in range(1, NZ):
                os_copy(1 - x, h, {"hidden": lax.rem(h + k, NZ)}, osr_send.at[k - 1]).start()

    n_end = per_round * (NZ - 1)
    n_across = 2 * (NC + N_W + N_A)
    units_e, units_m = N_E + (NZ - 1) * N_B, NC + N_W + 3 * M0

    def body(t, carry):
        @pl.when(end & ((t < PAUSE) | ((t >= PAUSE + HOLD) & (t < n_end + HOLD))))
        def _():
            end_z(t)

        @pl.when(mid)
        def _():
            mid_outer(t)

            @pl.when(t < n_across)
            def _():
                mid_across(t)

        n = t - LAG

        @pl.when((n >= 0) & (n < jnp.where(end, units_e, units_m)))
        def _():
            x_step(n)

        stages(t)
        return carry

    lax.fori_loop(0, max(n_end + HOLD, n_across, units_e + LAG, units_m + LAG), body, 0)

    send_parts(1, is_last)

    @pl.when(end)
    def _():
        pt_copy(0).wait_recv()
        acc[1, h] += PR[...].astype(jnp.float32)

    IS[x] = summed(1)
    is_copy(x).start()

    for k in range(1, NZ):
        for xx in range(2):
            os_copy(xx, lax.rem(h + k, NZ), {"ctx": 1 - x}, os_send.at[0]).wait_recv()

    total = lax.dot_general(OS[x], IS[x], NT, preferred_element_type=jnp.float32)
    is_copy(1 - x).wait_recv()
    total = total + lax.dot_general(OS[1 - x], IS[1 - x], NT, preferred_element_type=jnp.float32)
    out_ref[...] = jnp.dot(
        rot_ref[...], total.astype(jnp.bfloat16), preferred_element_type=jnp.float32)

    is_copy(x).wait_send()
    for k in range(NZ):
        os_copy(x, h, {"ctx": 1 - x}, os_send.at[k]).wait_send()
        if k:
            os_copy(x, h, {"ctx": 1 - x}, osr_send.at[k - 1]).wait_send()
    for to in range(NZ):
        @pl.when(h != to)
        def _(to=to):
            part(0, to, h).wait_send()
            part(1, to, h).wait_send()

    @pl.when(end)
    def _():
        sent(0, z, x, 0, NC)
        sent(0, z, 1 - x, A0, NC)
        for k in range(N_K):
            t_copy(k).wait_send()
        sent(2, z, x, 0, K0)
        sent(2, z, x, A0, NC)
        for r in range(1, NZ):
            sent(2, jnp.where(low, r, NZ - 1 - r), x, 0, K0)

    @pl.when(mid)
    def _():
        for zs in (z, outward):
            sent(0, zs, x, 0, NC)
            sent(0, zs, 1 - x, M0, NC)
        for zs in (z, inward, far):
            sent(1, zs, x, 0, K0)
            sent(1, zs, x, A0, NC)
            sent(1, zs, 1 - x, A0, NC)
        sent(2, z, x, 0, NC)
        sent(2, outward, x, 0, A0)
        sent(2, inward, x, 0, M0)
        sent(2, far, x, 0, M0)
        for to in range(NZ):
            @pl.when(h != to)
            def _(to=to):
                p_copy(to, h).wait_send()
        pt_copy(1).wait_send()


def fast(activations, out_grads, input_basis, output_basis, rotation):
    tokens = activations.reshape(-1, activations.shape[-1])
    grad_rows = out_grads.reshape(-1, out_grads.shape[-1])
    d_in, d_out = tokens.shape[1], grad_rows.shape[1]
    width = d_in + d_out
    m = tokens.shape[0]
    w = input_basis.shape[1]
    rank = rotation.shape[1]
    blk = 2 * w
    dma = pltpu.SemaphoreType.DMA
    f32, bf16 = jnp.float32, jnp.bfloat16
    anym = pl.BlockSpec(memory_space=pl.ANY)
    vmem = pl.BlockSpec(memory_space=pltpu.VMEM)
    logged = pl.pallas_call(
        kernel,
        out_shape=jax.ShapeDtypeStruct((rotation.shape[0], blk), f32),
        in_specs=[anym, anym, anym, anym, vmem],
        out_specs=vmem,
        scratch_shapes=[
            pltpu.VMEM((NZ, blk, width), bf16),
            pltpu.VMEM((m, width), bf16),
            pltpu.VMEM((2, NZ, blk, m), f32),
            pltpu.VMEM((NZ, blk, m), f32),
            pltpu.VMEM((NZ, blk, m), f32),
            pltpu.VMEM((2, rank, m), bf16),
            pltpu.VMEM((2, blk, m), bf16),
            pltpu.VMEM((m, width // NC * N_K), bf16),
            pltpu.VMEM((NZ, blk, m), f32),
            pltpu.VMEM((NZ, blk, m), bf16),
            pltpu.VMEM((NZ, blk, m), bf16),
            pltpu.VMEM((blk, m), bf16),
            pltpu.VMEM((blk, m), bf16),
            dma((3,)), dma((3,)), dma((NZ, 2, NC)), dma((3, NZ, 2)),
            dma((NZ,)), dma((NZ,)), dma((NZ,)), dma((NZ,)),
            dma((2, NZ)), dma((NZ,)), dma((NZ,)), dma((2,)),
            dma((N_K,)), dma((N_K,)), dma((NZ,)), dma((NZ,)), dma((2,)),
        ],
        compiler_params=pltpu.CompilerParams(
            collective_id=0, has_side_effects=True, vmem_limit_bytes=60 * 2**20),
    )(tokens, grad_rows, input_basis.T, output_basis.T, rotation)
    return logged.reshape(1, logged.shape[0], logged.shape[1])


def solution(mesh):
    size = mesh.shape

    def program(activations, out_grads, input_basis, output_basis, rotation):
        fits = (
            size["dp"] == NZ and size["hidden"] == NZ and size["ctx"] == 2
            and out_grads.shape[2] % (128 * N_OUT * NZ) == 0
            and activations.shape[2] * N_OUT == out_grads.shape[2] * (NC - N_OUT)
        )
        return jax.shard_map(
            fast if fits else local,
            mesh=mesh,
            in_specs=(
                P("dp", "ctx", "hidden"),
                P("dp", "ctx", "hidden"),
                P("hidden", ("dp", "ctx")),
                P("hidden", ("dp", "ctx")),
                P("ctx", None),
            ),
            out_specs=P("dp", "ctx", "hidden"),
            check_vma=False,
        )(activations, out_grads, input_basis, output_basis, rotation)

    return program
```
